256 devices in a mesh: dp: 4 (over x), cls: 64 (over z, y, core).
Axes of the slice: x: 4, y: 4, z: 8, core: 2. Of those that a mesh axis runs over, the one named last changes fastest.
Arguments:
- embeddings: float32 [2048, 512], P('dp'), may hold values from -60 to 60, as said below
- classifier: float32 [1048576, 512], P(('dp', 'cls')), may hold values from -60 to 60, as said below
- labels: int32 [2048], replicated, may hold values from 0 to 1048575
- row_scale: float32 [2048], replicated, may hold values from 16 to 512
Outputs:
- loss: float32 [2048], P(('dp', 'cls'))
The draws below stay inside these ranges and needn't reach their ends.
Inputs may be any that keep to these rules, and one draw needn't show every extreme that they name: `embeddings`: rows of different scales. `classifier`: rows of different scales.
All inputs are finite; a program needn't handle non-finite values.
Results may differ from the reference program's by a relative error of at most 0.0003.
Values sent between devices are 32-bit elements; how exact they have to be, the bound alone decides.
No kernel may reach another device: no remote copies, remote signals or barrier semaphores. Data moves between devices by JAX's collectives and lax.ppermute only.
A program may use at most 128 MiB of HBM per device.

```python
import math
import jax
import jax.numpy as jnp
from jax import lax

D = 512
CLS_DEV = 4096
EMBEDS = 2048
CLASSES = 1048576


def class_row(base, index):
    row_key = jax.random.fold_in(base, index)
    return jax.random.truncated_normal(row_key, -6.0, 6.0, (D,), jnp.float32)


def many_rows(base, indices):

    def single(index):
        return class_row(base, index)
    return jax.vmap(single)(indices)


def draw_classifier(key, part):
    base = jax.random.fold_in(key, 101)
    rows = many_rows(base, jnp.arange(CLASSES, dtype=jnp.int32))
    scales = jnp.exp(jax.random.uniform(jax.random.fold_in(key, 102), (CLASSES, 1), jnp.float32, 0.0, math.log(10.0)))
    return rows * scales


def draw_embeddings(key, part):
    scales = jnp.exp(jax.random.uniform(jax.random.fold_in(key, 202), (EMBEDS, 1), jnp.float32, 0.0, math.log(10.0)))
    noise = jax.random.truncated_normal(jax.random.fold_in(key, 201), -6.0, 6.0, (EMBEDS, D), jnp.float32)
    return noise * scales


def with_ends(values, key, least, high):
    shape = values.shape
    spot = [jax.random.randint(jax.random.fold_in(key, axis), (), 0, shape[axis]) for axis in range(len(shape))]
    values = values.at[tuple(spot)].set(least)
    longest = shape.index(max(shape))
    spot[longest] = (spot[longest] + 1) % shape[longest]
    return values.at[tuple(spot)].set(high)


def setup_inputs(seed: int = 0) -> dict:
    keys = jax.random.split(jax.random.key(seed), 5)
    return {
        "embeddings": draw_embeddings(jax.random.fold_in(keys[4], 71), 0),
        "classifier": draw_classifier(jax.random.fold_in(keys[4], 71), 0),
        "labels": with_ends(jax.random.randint(keys[2], (EMBEDS,), 0, CLASSES), jax.random.fold_in(keys[2], 1), 0, CLASSES - 1).astype(jnp.int32),
        "row_scale": jnp.clip(jnp.exp(jax.random.uniform(keys[3], (EMBEDS,), jnp.float32, math.log(16.0), math.log(512.0))), 16.0, 512.0),
    }


MARGIN = 0.5
COS_MARGIN = math.cos(MARGIN)
SIN_MARGIN = math.sin(MARGIN)

def unit_rows(values):
    return values * lax.rsqrt(lax.optimization_barrier(jnp.sum(values * values, axis=-1, keepdims=True)) + 1e-06)

def margin_logit(units, picked, scales):
    cosine = lax.optimization_barrier(jnp.sum(units * picked, axis=-1))
    across = units - cosine[:, None] * picked
    sine = jnp.sqrt(lax.optimization_barrier(jnp.sum(across * across, axis=-1)))
    return scales * (cosine * COS_MARGIN - sine * SIN_MARGIN)

def block_stats(units, rows, class_ids, labels, scales, picked, owned):
    cosine = lax.dot_general(units, rows, (((1,), (1,)), ((), ())), precision=lax.Precision.HIGHEST, preferred_element_type=jnp.float32)
    target = margin_logit(units, picked, scales)
    hit = labels[:, None] == class_ids[None, :]
    logits = jnp.where(hit, target[:, None], scales[:, None] * cosine)
    peak = lax.optimization_barrier(jnp.max(logits, axis=1))
    total = lax.optimization_barrier(jnp.sum(jnp.exp(logits - peak[:, None]), axis=1))
    return (peak, total, jnp.where(owned, target, jnp.zeros_like(target)))

def merge_rows(first, second):
    peak = jnp.maximum(first[0], second[0])
    total = first[1] * jnp.exp(first[0] - peak) + second[1] * jnp.exp(second[0] - peak)
    return (peak, total, first[2] + second[2])

def reference(embeddings, classifier, labels, row_scale):
    units = unit_rows(embeddings)
    count = CLASSES // CLS_DEV
    blocks = classifier.reshape(count, CLS_DEV, D)
    numbers = jnp.arange(count).astype(jnp.int32)

    def step(carry, item):
        block, number = item
        normed = unit_rows(block)
        offset = number * CLS_DEV
        class_ids = offset + jnp.arange(CLS_DEV).astype(jnp.int32)
        owned = (labels >= offset) & (labels < offset + CLS_DEV)
        local = jnp.clip(labels - offset, 0, CLS_DEV - 1).astype(jnp.int32)
        picked = jnp.take(normed, local, axis=0)
        stats = block_stats(units, normed, class_ids, labels, row_scale, picked, owned)
        return (merge_rows(carry, stats), None)
    start = jnp.full((EMBEDS,), -1e+30, jnp.float32)
    empty = jnp.zeros((EMBEDS,), jnp.float32)
    (peak, total, target), unused = lax.scan(step, (start, empty, empty), (blocks, numbers))
    return peak + jnp.log(total) - target
```

```python
import functools
import math

import jax
import jax.numpy as jnp
from jax import lax
from jax.experimental import pallas as pl
from jax.experimental.pallas import tpu as pltpu
from jax.sharding import Mesh
from jax.sharding import PartitionSpec as P

DP_CLS = ("dp", "cls_0", "cls_1", "cls_2")


MARGIN = 0.5
COS_MARGIN = math.cos(MARGIN)
SIN_MARGIN = math.sin(MARGIN)
EPS = 1e-06
LOG2E = math.log2(math.e)
LN2 = math.log(2.0)
LOWEST = -3e38

HALF = 256
TILE = 1024
SUB = 128
SLOTS = 32


def split(values):
    high = values.astype(jnp.bfloat16)
    return high, (values - high.astype(jnp.float32)).astype(jnp.bfloat16)


def owned_kernel(meta_ref, labels_ref, list_ref, *, rows_here):
    local = labels_ref[...] - meta_ref[2]
    lines, lanes = local.shape
    count = lines * lanes
    number = lax.broadcasted_iota(jnp.int32, local.shape, 0) * lanes
    number = number + lax.broadcasted_iota(jnp.int32, local.shape, 1)
    number = jnp.where((local >= 0) & (local < rows_here), number, count)

    def more(state):
        return state[1] < count

    def step(state):
        found, at = state
        list_ref[found] = at
        return found + 1, jnp.min(jnp.where(number > at, number, count))

    found, _ = lax.while_loop(more, step, (jnp.int32(0), jnp.min(number)))
    list_ref[count] = found


def owned(meta, labels, rows_here):
    count = labels.shape[0]
    return pl.pallas_call(
        functools.partial(owned_kernel, rows_here=rows_here),
        in_specs=[pl.BlockSpec(memory_space=pltpu.SMEM), pl.BlockSpec(memory_space=pltpu.VMEM)],
        out_specs=pl.BlockSpec(memory_space=pltpu.SMEM),
        out_shape=jax.ShapeDtypeStruct((count + 128,), jnp.int32),
        name="owned",
    )(meta, labels.reshape(-1, 128))


def half_ids(meta_ref, shift, ways):
    block = lax.rem(meta_ref[0] + (ways - shift), ways)
    swap = jnp.int32(0) if shift == 0 else meta_ref[1]
    return 2 * block + swap, 2 * block + 1 - swap


def start_target(k, number, meta_ref, labels_ref, rows_ref, sources, ways, found_ref, picked_ref, sems):
    place, core, offset = meta_ref[0], meta_ref[1], meta_ref[2]
    local = labels_ref[number] - offset
    at = pl.multiple_of((local // 8) * 8, 8)
    pltpu.make_async_copy(rows_ref.at[pl.ds(at, 8), :], picked_ref.at[k], sems.at[1, k]).start()
    half = number // HALF
    shift = lax.rem(place + ways - half // 2, ways)
    swapped = jnp.where(lax.rem(half, 2) == core, 0, 1)
    for (s, w), ref in sources.items():
        here = shift == s
        if w is not None:
            here = here & (swapped == w)

        @pl.when(here)
        def _(ref=ref):
            from_row = pl.multiple_of((lax.rem(number, ref.shape[0]) // 8) * 8, 8)
            pltpu.make_async_copy(ref.at[pl.ds(from_row, 8), :], found_ref.at[k], sems.at[0, k]).start()


def stats_kernel(meta_ref, *refs, shifts, ways, first, last):
    refs = list(refs)
    take = lambda n: [refs.pop(0) for _ in range(n)]
    labels_ref, scales_ref = take(2)
    halves = take(len(shifts) if first else 2 * len(shifts))
    if first:
        (rows_ref,) = take(1)
    else:
        high_ref, low_ref, before_ref = take(3)
    if last:
        list_ref, flat_labels_ref, flat_scales_ref, all_rows_ref = take(4)
        sources = {(0, None): refs.pop(0)}
        for s in range(1, ways):
            for w in range(2):
                sources[(s, w)] = refs.pop(0)
    (out_ref,) = take(1)
    if first:
        high_ref, low_ref = take(2)
    raw_ref, uh_ref, ul_ref, peak_ref, total_ref, local_ref, raw_sems = take(7)
    if last:
        found_ref, picked_ref, sems = take(3)
    step = pl.program_id(0)
    offset = meta_ref[2]
    ids = [i for s in shifts for i in half_ids(meta_ref, s, ways)]

    if last:
        limit = flat_labels_ref.shape[0]

        def begin(base, here):
            def one(k, carry):
                number = list_ref[base + k]
                start_target(
                    k, number, meta_ref, flat_labels_ref, all_rows_ref, sources, ways, found_ref, picked_ref, sems
                )
                return carry

            lax.fori_loop(0, here, one, 0)

        def finish(base, here):
            def wait(k, carry):
                rows = all_rows_ref.at[pl.ds(0, 8), :]
                pltpu.make_async_copy(rows, found_ref.at[k], sems.at[0, k]).wait()
                pltpu.make_async_copy(rows, picked_ref.at[k], sems.at[1, k]).wait()
                return carry

            lax.fori_loop(0, here, wait, 0)

            def one(k, carry):
                number = list_ref[base + k]
                local = flat_labels_ref[number] - offset
                values = found_ref[k, pl.ds(lax.rem(number, 8), 1), :]
                row = picked_ref[k, pl.ds(lax.rem(local, 8), 1), :]
                units = values * lax.rsqrt(jnp.sum(values * values, axis=1, keepdims=True) + EPS)
                row = row * lax.rsqrt(jnp.sum(row * row, axis=1, keepdims=True) + EPS)
                cosine = jnp.sum(units * row, axis=1, keepdims=True)
                across = units - cosine * row
                sine = jnp.sqrt(jnp.sum(across * across, axis=1, keepdims=True))
                target = flat_scales_ref[number] * (cosine * COS_MARGIN - sine * SIN_MARGIN)
                line = out_ref[number // HALF, pl.ds(1, 1), :]
                lane = lax.broadcasted_iota(jnp.int32, line.shape, 1)
                out_ref[number // HALF, pl.ds(1, 1), :] = jnp.where(lane == lax.rem(number, HALF), target, line)
                return carry

            lax.fori_loop(0, here, one, 0)

    @pl.when(step == 0)
    def _():
        if first:
            loads = [pltpu.make_async_copy(halves[0], raw_ref, raw_sems.at[0])]
        else:
            loads = [
                pltpu.make_async_copy(ref, raw_ref.at[pl.ds(h * HALF, HALF), :], raw_sems.at[h])
                for h, ref in enumerate(halves)
            ]
        for load in loads:
            load.start()
        if last:
            begin(0, jnp.minimum(list_ref[limit], SLOTS))
        for h in range(2 * len(shifts)):
            if h < len(loads):
                loads[h].wait()
            at = slice(h * HALF, (h + 1) * HALF)
            values = raw_ref[at, :].T
            inverse = lax.rsqrt(jnp.sum(values * values, axis=0, keepdims=True) + EPS)
            high, low = split(values * inverse * (scales_ref[ids[h]] * LOG2E))
            uh_ref[:, at] = high
            ul_ref[:, at] = low
            local_ref[:, at] = labels_ref[ids[h]] - offset
        peak_ref[...] = jnp.full_like(peak_ref, LOWEST)
        total_ref[...] = jnp.zeros_like(total_ref)

    peak, total = peak_ref[...], total_ref[...]
    width = peak.shape[1]
    uh, ul = uh_ref[...], ul_ref[...]
    local = jnp.broadcast_to(local_ref[...] - step * TILE, (8, width))
    local = local - lax.broadcasted_iota(jnp.int32, (8, width), 0)
    for k in range(TILE // SUB):
        at = slice(k * SUB, (k + 1) * SUB)
        if first:
            rows = rows_ref[at, :]
            rows = rows * lax.rsqrt(jnp.sum(rows * rows, axis=1, keepdims=True) + EPS)
            high, low = split(rows)
            high_ref[at, :] = high
            low_ref[at, :] = low
        else:
            high, low = high_ref[at, :], low_ref[at, :]
        logits = jnp.dot(high, uh, preferred_element_type=jnp.float32)
        logits = logits + jnp.dot(low, uh, preferred_element_type=jnp.float32)
        logits = logits + jnp.dot(high, ul, preferred_element_type=jnp.float32)
        parts = [
            jnp.where(local == k * SUB + 8 * g, LOWEST, logits[8 * g : 8 * g + 8]) for g in range(SUB // 8)
        ]
        tops = list(parts)
        while len(tops) > 1:
            tops = [jnp.maximum(a, b) for a, b in zip(tops[::2], tops[1::2])]
        above = jnp.maximum(peak, tops[0])
        sums = [jnp.exp2(part - above) for part in parts]
        while len(sums) > 1:
            sums = [a + b for a, b in zip(sums[::2], sums[1::2])]
        total = total * jnp.exp2(peak - above) + sums[0]
        peak = above
    peak_ref[...] = peak
    total_ref[...] = total

    @pl.when(step == pl.num_programs(0) - 1)
    def _():
        top = jnp.max(peak, axis=0, keepdims=True)
        full = jnp.sum(total * jnp.exp2(peak - top), axis=0, keepdims=True)
        level = top + jnp.log2(full)
        if first:
            out_ref[...] = jnp.zeros_like(out_ref)
        else:
            out_ref[...] = before_ref[...]
        for h, i in enumerate(ids):
            out_ref[i, pl.ds(0, 1), :] = level[:, h * HALF : (h + 1) * HALF]
        if last:
            found = list_ref[limit]
            finish(0, jnp.minimum(found, SLOTS))

            def batch(b, carry):
                here = jnp.minimum(found - b * SLOTS, SLOTS)
                begin(b * SLOTS, here)
                finish(b * SLOTS, here)
                return carry

            lax.fori_loop(1, (found + SLOTS - 1) // SLOTS, batch, 0)


def stats(meta, labels, scales, shifts, halves, rows, ways, before=None, extra=None):
    first, last = before is None, extra is not None
    rows_here, width = rows[0].shape
    blocks = labels.shape[0]
    lines = 2 * HALF * len(shifts)
    whole = lambda *shape: pl.BlockSpec(shape, lambda t, meta: (0,) * len(shape))
    far = pl.BlockSpec(memory_space=pl.ANY)
    scalars = pl.BlockSpec(memory_space=pltpu.SMEM)
    tiles = pl.BlockSpec((TILE, width), lambda t, meta: (t, 0))
    in_specs = [whole(blocks, 1, HALF), whole(blocks, 1, HALF)] + [far] * len(halves) + [tiles] * len(rows)
    args = [labels, scales, *halves, *rows]
    out_specs = [whole(blocks, 2, HALF)]
    out_shape = [jax.ShapeDtypeStruct((blocks, 2, HALF), jnp.float32)]
    scratch = [
        pltpu.VMEM((lines, width), jnp.float32),
        pltpu.VMEM((width, lines), jnp.bfloat16),
        pltpu.VMEM((width, lines), jnp.bfloat16),
        pltpu.VMEM((8, lines), jnp.float32),
        pltpu.VMEM((8, lines), jnp.float32),
        pltpu.VMEM((1, lines), jnp.int32),
        pltpu.SemaphoreType.DMA((2 * len(shifts),)),
    ]
    if first:
        out_specs += [tiles, tiles]
        out_shape += [jax.ShapeDtypeStruct((rows_here, width), jnp.bfloat16)] * 2
    else:
        in_specs.append(whole(blocks, 2, HALF))
        args.append(before)
    if last:
        in_specs += [scalars] * 3 + [far] * (len(extra) - 3)
        args += extra
        scratch += [
            pltpu.VMEM((SLOTS, 8, width), jnp.float32),
            pltpu.VMEM((SLOTS, 8, width), jnp.float32),
            pltpu.SemaphoreType.DMA((2, SLOTS)),
        ]
    return pl.pallas_call(
        functools.partial(stats_kernel, shifts=shifts, ways=ways, first=first, last=last),
        grid_spec=pltpu.PrefetchScalarGridSpec(
            num_scalar_prefetch=1,
            grid=(rows_here // TILE,),
            in_specs=in_specs,
            out_specs=out_specs,
            scratch_shapes=scratch,
        ),
        out_shape=out_shape,
        compiler_params=pltpu.CompilerParams(dimension_semantics=("arbitrary",)),
    )(meta, *args)


def body(embeddings, classifier, labels, row_scale):
    rows_here = classifier.shape[0]
    count = labels.shape[0]
    ways = lax.axis_size("dp")
    core = lax.axis_index("cls_2")
    meta = jnp.stack([lax.axis_index("dp"), core, lax.axis_index(DP_CLS) * rows_here]).astype(jnp.int32)
    swap = lambda part: lax.ppermute(part, "cls_2", [(0, 1), (1, 0)])
    shift = lambda part, k: lax.ppermute(part, "dp", [(i, (i + k) % ways) for i in range(ways)])

    label_blocks = labels.reshape(-1, 1, HALF)
    scale_blocks = row_scale.reshape(-1, 1, HALF)
    mine = lax.dynamic_slice_in_dim(embeddings, core * HALF, HALF, 0)
    left = shift(mine, 1)
    right = shift(mine, 3)
    across = shift(mine, 2)
    numbers = owned(meta, labels, rows_here)
    held, high, low = stats(meta, label_blocks, scale_blocks, (0,), (embeddings,), (classifier,), ways)
    near = (left, swap(left), right, swap(right))
    (held,) = stats(meta, label_blocks, scale_blocks, (1, 3), near, (high, low), ways, held)
    far = (across, swap(across))
    extra = [numbers, labels, row_scale, classifier, embeddings, near[0], near[1], *far, near[2], near[3]]
    (held,) = stats(meta, label_blocks, scale_blocks, (2,), far, (high, low), ways, held, extra)

    devices = lax.axis_size(DP_CLS)
    share = count // devices
    send = held.reshape(-1, 2, HALF // share, share).transpose(0, 2, 1, 3).reshape(devices, 2 * share)
    got = lax.all_to_all(send, DP_CLS, 0, 0, tiled=True)
    level, target = got[:, :share], jnp.sum(got[:, share:], axis=0)
    top = jnp.max(level, axis=0)
    peak = jnp.maximum(top * LN2, target)
    total = jnp.sum(jnp.exp2(level - top), axis=0) * jnp.exp(top * LN2 - peak) + jnp.exp(target - peak)
    return peak + jnp.log(total) - target


def solution(mesh):
    torus = Mesh(mesh.devices.reshape(mesh.shape["dp"], 8, 4, 2), ("dp", "cls_0", "cls_1", "cls_2"))
    return jax.shard_map(
        body,
        mesh=torus,
        in_specs=(P("dp", None), P(DP_CLS, None), P(), P()),
        out_specs=P(DP_CLS),
        check_vma=False,
    )
```

```python
import functools
import math

import jax
import jax.numpy as jnp
from jax import lax
from jax.experimental import pallas as pl
from jax.experimental.pallas import tpu as pltpu
from jax.sharding import Mesh
from jax.sharding import PartitionSpec as P

DP_CLS = ("dp", "cls_0", "cls_1", "cls_2")


MARGIN = 0.5
COS_MARGIN = math.cos(MARGIN)
SIN_MARGIN = math.sin(MARGIN)
EPS = 1e-06
LOG2E = math.log2(math.e)
LN2 = math.log(2.0)
LOWEST = -3e38

HALF = 256
TILE = 1024
SUB = 256
SLOTS = 32
CHAINS = 4


def split(values):
    high = values.astype(jnp.bfloat16)
    return high, (values - high.astype(jnp.float32)).astype(jnp.bfloat16)


def product(a, b):
    return lax.dot_general(a, b, (((1,), (1,)), ((), ())), preferred_element_type=jnp.float32)


def owned_kernel(meta_ref, labels_ref, list_ref, *, rows_here):
    local = labels_ref[...] - meta_ref[2]
    lines, lanes = local.shape
    count = lines * lanes
    number = lax.broadcasted_iota(jnp.int32, local.shape, 0) * lanes
    number = number + lax.broadcasted_iota(jnp.int32, local.shape, 1)
    number = jnp.where((local >= 0) & (local < rows_here), number, count)

    chains = [number[q * lines // CHAINS : (q + 1) * lines // CHAINS] for q in range(CHAINS)]

    def step(state):
        found, heads = state
        for head in heads:
            here = head < count

            @pl.when(here)
            def _(found=found, head=head):
                list_ref[found] = head

            found = found + here.astype(jnp.int32)
        return found, [jnp.min(jnp.where(part > head, part, count)) for part, head in zip(chains, heads)]

    def more(state):
        return functools.reduce(jnp.minimum, state[1]) < count

    found, _ = lax.while_loop(more, step, (jnp.int32(0), [jnp.min(part) for part in chains]))
    list_ref[count] = found


def owned(meta, labels, rows_here):
    count = labels.shape[0]
    return pl.pallas_call(
        functools.partial(owned_kernel, rows_here=rows_here),
        in_specs=[pl.BlockSpec(memory_space=pltpu.SMEM), pl.BlockSpec(memory_space=pltpu.VMEM)],
        out_specs=pl.BlockSpec(memory_space=pltpu.SMEM),
        out_shape=jax.ShapeDtypeStruct((count + 128,), jnp.int32),
        name="owned",
    )(meta, labels.reshape(-1, 128))


def half_ids(meta_ref, shift, ways):
    block = lax.rem(meta_ref[0] + (ways - shift), ways)
    swap = jnp.int32(0) if shift == 0 else meta_ref[1]
    return 2 * block + swap, 2 * block + 1 - swap


def start_target(k, number, meta_ref, labels_ref, rows_ref, sources, ways, found_ref, picked_ref, sems):
    place, core, offset = meta_ref[0], meta_ref[1], meta_ref[2]
    local = labels_ref[number] - offset
    at = pl.multiple_of((local // 8) * 8, 8)
    pltpu.make_async_copy(rows_ref.at[pl.ds(at, 8), :], picked_ref.at[k], sems.at[1, k]).start()
    half = number // HALF
    shift = lax.rem(place + ways - half // 2, ways)
    swapped = jnp.where(lax.rem(half, 2) == core, 0, 1)
    for (s, w), ref in sources.items():
        here = shift == s
        if w is not None:
            here = here & (swapped == w)

        @pl.when(here)
        def _(ref=ref):
            from_row = pl.multiple_of((lax.rem(number, ref.shape[0]) // 8) * 8, 8)
            pltpu.make_async_copy(ref.at[pl.ds(from_row, 8), :], found_ref.at[k], sems.at[0, k]).start()


def stats_kernel(meta_ref, *refs, shifts, ways, first, last):
    refs = list(refs)
    take = lambda n: [refs.pop(0) for _ in range(n)]
    labels_ref, scales_ref = take(2)
    halves = take(len(shifts) if first else 2 * len(shifts))
    if first:
        (rows_ref,) = take(1)
    else:
        high_ref, low_ref, before_ref = take(3)
    if last:
        list_ref, flat_labels_ref, flat_scales_ref, all_rows_ref = take(4)
        sources = {(0, None): refs.pop(0)}
        for s in range(1, ways):
            for w in range(2):
                sources[(s, w)] = refs.pop(0)
    (out_ref,) = take(1)
    if first:
        high_ref, low_ref = take(2)
    raw_ref, uh_ref, ul_ref, peak_ref, total_ref, local_ref, raw_sems = take(7)
    if last:
        found_ref, picked_ref, group_ref, sems = take(4)
    step = pl.program_id(0)
    offset = meta_ref[2]
    ids = [i for s in shifts for i in half_ids(meta_ref, s, ways)]

    if last:
        limit = flat_labels_ref.shape[0]

        def begin(base, here):
            def one(k, carry):
                number = list_ref[base + k]
                start_target(
                    k, number, meta_ref, flat_labels_ref, all_rows_ref, sources, ways, found_ref, picked_ref, sems
                )
                return carry

            lax.fori_loop(0, here, one, 0)

        def finish(base, here):
            def wait(k, carry):
                rows = all_rows_ref.at[pl.ds(0, 8), :]
                pltpu.make_async_copy(rows, found_ref.at[k], sems.at[0, k]).wait()
                pltpu.make_async_copy(rows, picked_ref.at[k], sems.at[1, k]).wait()
                return carry

            lax.fori_loop(0, here, wait, 0)

            def eight(g, carry):
                first_slot = g * 8
                numbers = []
                for k in range(8):
                    slot = first_slot + k
                    number = jnp.where(slot < here, list_ref[base + slot], 0)
                    local = jnp.maximum(flat_labels_ref[number] - offset, 0)
                    group_ref[0, k : k + 1, :] = found_ref[slot, pl.ds(lax.rem(number, 8), 1), :]
                    group_ref[1, k : k + 1, :] = picked_ref[slot, pl.ds(lax.rem(local, 8), 1), :]
                    numbers.append(number)
                units, picked = group_ref[0], group_ref[1]
                units = units * lax.rsqrt(jnp.sum(units * units, axis=1, keepdims=True) + EPS)
                picked = picked * lax.rsqrt(jnp.sum(picked * picked, axis=1, keepdims=True) + EPS)
                cosine = jnp.sum(units * picked, axis=1, keepdims=True)
                across = units - cosine * picked
                sine = jnp.sqrt(jnp.sum(across * across, axis=1, keepdims=True))
                margin = cosine * COS_MARGIN - sine * SIN_MARGIN
                for k in range(8):
                    number = numbers[k]

                    @pl.when(first_slot + k < here)
                    def _(k=k, number=number):
                        target = flat_scales_ref[number] * margin[k : k + 1]
                        line = out_ref[number // HALF, pl.ds(1, 1), :]
                        lane = lax.broadcasted_iota(jnp.int32, line.shape, 1)
                        line = jnp.where(lane == lax.rem(number, HALF), target, line)
                        out_ref[number // HALF, pl.ds(1, 1), :] = line

                return carry

            lax.fori_loop(0, (here + 7) // 8, eight, 0)

    @pl.when(step == 0)
    def _():
        if first:
            loads = [pltpu.make_async_copy(halves[0], raw_ref, raw_sems.at[0])]
        else:
            loads = [
                pltpu.make_async_copy(ref, raw_ref.at[pl.ds(h * HALF, HALF), :], raw_sems.at[h])
                for h, ref in enumerate(halves)
            ]
        for load in loads:
            load.start()
        if last:
            begin(0, jnp.minimum(list_ref[limit], SLOTS))
        for h in range(2 * len(shifts)):
            if h < len(loads):
                loads[h].wait()
            at = slice(h * HALF, (h + 1) * HALF)
            values = raw_ref[at, :]
            inverse = lax.rsqrt(jnp.sum(values * values, axis=1, keepdims=True) + EPS)
            scale = jnp.broadcast_to(scales_ref[ids[h]] * LOG2E, (8, HALF)).T[:, :1]
            high, low = split(values * (inverse * scale))
            uh_ref[at, :] = high
            ul_ref[at, :] = low
            local_ref[:, at] = labels_ref[ids[h]] - offset
        peak_ref[...] = jnp.full_like(peak_ref, LOWEST)
        total_ref[...] = jnp.zeros_like(total_ref)

    peak, total = peak_ref[...], total_ref[...]
    width = peak.shape[1]
    uh, ul = uh_ref[...], ul_ref[...]
    local = jnp.broadcast_to(local_ref[...] - step * TILE, (8, width))
    local = local - lax.broadcasted_iota(jnp.int32, (8, width), 0)
    for k in range(TILE // SUB):
        at = slice(k * SUB, (k + 1) * SUB)
        if first:
            rows = rows_ref[at, :]
            rows = rows * lax.rsqrt(jnp.sum(rows * rows, axis=1, keepdims=True) + EPS)
            high, low = split(rows)
            high_ref[at, :] = high
            low_ref[at, :] = low
        else:
            high, low = high_ref[at, :], low_ref[at, :]
        logits = product(high, uh) + product(low, uh) + product(high, ul)
        parts = [
            jnp.where(local == k * SUB + 8 * g, LOWEST, logits[8 * g : 8 * g + 8]) for g in range(SUB // 8)
        ]
        tops = list(parts)
        while len(tops) > 1:
            tops = [jnp.maximum(a, b) for a, b in zip(tops[::2], tops[1::2])]
        above = jnp.maximum(peak, tops[0])
        sums = [jnp.exp2(part - above) for part in parts]
        while len(sums) > 1:
            sums = [a + b for a, b in zip(sums[::2], sums[1::2])]
        total = total * jnp.exp2(peak - above) + sums[0]
        peak = above
    peak_ref[...] = peak
    total_ref[...] = total

    @pl.when(step == pl.num_programs(0) - 1)
    def _():
        top = jnp.max(peak, axis=0, keepdims=True)
        full = jnp.sum(total * jnp.exp2(peak - top), axis=0, keepdims=True)
        level = top + jnp.log2(full)
        if first:
            out_ref[...] = jnp.zeros_like(out_ref)
        else:
            out_ref[...] = before_ref[...]
        for h, i in enumerate(ids):
            out_ref[i, pl.ds(0, 1), :] = level[:, h * HALF : (h + 1) * HALF]
        if last:
            found = list_ref[limit]
            finish(0, jnp.minimum(found, SLOTS))

            def batch(b, carry):
                here = jnp.minimum(found - b * SLOTS, SLOTS)
                begin(b * SLOTS, here)
                finish(b * SLOTS, here)
                return carry

            lax.fori_loop(1, (found + SLOTS - 1) // SLOTS, batch, 0)


def stats(meta, labels, scales, shifts, halves, rows, ways, before=None, extra=None):
    first, last = before is None, extra is not None
    rows_here, width = rows[0].shape
    blocks = labels.shape[0]
    lines = 2 * HALF * len(shifts)
    whole = lambda *shape: pl.BlockSpec(shape, lambda t, meta: (0,) * len(shape))
    far = pl.BlockSpec(memory_space=pl.ANY)
    scalars = pl.BlockSpec(memory_space=pltpu.SMEM)
    tiles = pl.BlockSpec((TILE, width), lambda t, meta: (t, 0))
    in_specs = [whole(blocks, 1, HALF), whole(blocks, 1, HALF)] + [far] * len(halves) + [tiles] * len(rows)
    args = [labels, scales, *halves, *rows]
    out_specs = [whole(blocks, 2, HALF)]
    out_shape = [jax.ShapeDtypeStruct((blocks, 2, HALF), jnp.float32)]
    scratch = [
        pltpu.VMEM((lines, width), jnp.float32),
        pltpu.VMEM((lines, width), jnp.bfloat16),
        pltpu.VMEM((lines, width), jnp.bfloat16),
        pltpu.VMEM((8, lines), jnp.float32),
        pltpu.VMEM((8, lines), jnp.float32),
        pltpu.VMEM((1, lines), jnp.int32),
        pltpu.SemaphoreType.DMA((2 * len(shifts),)),
    ]
    if first:
        out_specs += [tiles, tiles]
        out_shape += [jax.ShapeDtypeStruct((rows_here, width), jnp.bfloat16)] * 2
    else:
        in_specs.append(whole(blocks, 2, HALF))
        args.append(before)
    if last:
        in_specs += [scalars] * 3 + [far] * (len(extra) - 3)
        args += extra
        scratch += [
            pltpu.VMEM((SLOTS, 8, width), jnp.float32),
            pltpu.VMEM((SLOTS, 8, width), jnp.float32),
            pltpu.VMEM((2, 8, width), jnp.float32),
            pltpu.SemaphoreType.DMA((2, SLOTS)),
        ]
    return pl.pallas_call(
        functools.partial(stats_kernel, shifts=shifts, ways=ways, first=first, last=last),
        grid_spec=pltpu.PrefetchScalarGridSpec(
            num_scalar_prefetch=1,
            grid=(rows_here // TILE,),
            in_specs=in_specs,
            out_specs=out_specs,
            scratch_shapes=scratch,
        ),
        out_shape=out_shape,
        compiler_params=pltpu.CompilerParams(dimension_semantics=("arbitrary",)),
    )(meta, *args)


def body(embeddings, classifier, labels, row_scale):
    rows_here = classifier.shape[0]
    count = labels.shape[0]
    ways = lax.axis_size("dp")
    core = lax.axis_index("cls_2")
    meta = jnp.stack([lax.axis_index("dp"), core, lax.axis_index(DP_CLS) * rows_here]).astype(jnp.int32)
    swap = lambda part: lax.ppermute(part, "cls_2", [(0, 1), (1, 0)])
    shift = lambda part, k: lax.ppermute(part, "dp", [(i, (i + k) % ways) for i in range(ways)])

    label_blocks = labels.reshape(-1, 1, HALF)
    scale_blocks = row_scale.reshape(-1, 1, HALF)
    mine = lax.dynamic_slice_in_dim(embeddings, core * HALF, HALF, 0)
    left = shift(mine, 1)
    right = shift(mine, 3)
    across = shift(mine, 2)
    numbers = owned(meta, labels, rows_here)
    held, high, low = stats(meta, label_blocks, scale_blocks, (0,), (embeddings,), (classifier,), ways)
    left_other = swap(left)
    near = (left, left_other, right, swap(right))
    (held,) = stats(meta, label_blocks, scale_blocks, (1, 3), near, (high, low), ways, held)
    far = (across, swap(across))
    extra = [numbers, labels, row_scale, classifier, embeddings, near[0], near[1], *far, near[2], near[3]]
    (held,) = stats(meta, label_blocks, scale_blocks, (2,), far, (high, low), ways, held, extra)

    devices = lax.axis_size(DP_CLS)
    share = count // devices
    send = held.reshape(-1, 2, HALF // share, share).transpose(0, 2, 1, 3).reshape(devices, 2 * share)
    got = lax.all_to_all(send, DP_CLS, 0, 0, tiled=True)
    level, target = got[:, :share], jnp.sum(got[:, share:], axis=0)
    top = jnp.max(level, axis=0)
    peak = jnp.maximum(top * LN2, target)
    total = jnp.sum(jnp.exp2(level - top), axis=0) * jnp.exp(top * LN2 - peak) + jnp.exp(target - peak)
    return peak + jnp.log(total) - target


def solution(mesh):
    torus = Mesh(mesh.devices.reshape(mesh.shape["dp"], 8, 4, 2), ("dp", "cls_0", "cls_1", "cls_2"))
    return jax.shard_map(
        body,
        mesh=torus,
        in_specs=(P("dp", None), P(DP_CLS, None), P(), P()),
        out_specs=P(DP_CLS),
        check_vma=False,
    )
```

```python
import functools
import math

import jax
import jax.numpy as jnp
from jax import lax
from jax.experimental import pallas as pl
from jax.experimental.pallas import tpu as pltpu
from jax.sharding import Mesh
from jax.sharding import PartitionSpec as P

DP_CLS = ("dp", "cls_0", "cls_1", "cls_2")


MARGIN = 0.5
COS_MARGIN = math.cos(MARGIN)
SIN_MARGIN = math.sin(MARGIN)
EPS = 1e-06
LOG2E = math.log2(math.e)
LN2 = math.log(2.0)
LOWEST = -3e38

HALF = 256
TILE = 1024
SUB = 256
SLOTS = 32
CHAINS = 4


def split(values):
    high = values.astype(jnp.bfloat16)
    return high, (values - high.astype(jnp.float32)).astype(jnp.bfloat16)


def product(a, b):
    return lax.dot_general(a, b, (((1,), (1,)), ((), ())), preferred_element_type=jnp.float32)


def owned_kernel(meta_ref, labels_ref, list_ref, *, rows_here):
    local = labels_ref[...] - meta_ref[2]
    lines, lanes = local.shape
    count = lines * lanes
    number = lax.broadcasted_iota(jnp.int32, local.shape, 0) * lanes
    number = number + lax.broadcasted_iota(jnp.int32, local.shape, 1)
    number = jnp.where((local >= 0) & (local < rows_here), number, count)

    chains = [number[q * lines // CHAINS : (q + 1) * lines // CHAINS] for q in range(CHAINS)]

    def step(state):
        found, heads = state
        for head in heads:
            here = head < count

            @pl.when(here)
            def _(found=found, head=head):
                list_ref[found] = head

            found = found + here.astype(jnp.int32)
        return found, [jnp.min(jnp.where(part > head, part, count)) for part, head in zip(chains, heads)]

    def more(state):
        return functools.reduce(jnp.minimum, state[1]) < count

    found, _ = lax.while_loop(more, step, (jnp.int32(0), [jnp.min(part) for part in chains]))
    list_ref[count] = found


def owned(meta, labels, rows_here):
    count = labels.shape[0]
    return pl.pallas_call(
        functools.partial(owned_kernel, rows_here=rows_here),
        in_specs=[pl.BlockSpec(memory_space=pltpu.SMEM), pl.BlockSpec(memory_space=pltpu.VMEM)],
        out_specs=pl.BlockSpec(memory_space=pltpu.SMEM),
        out_shape=jax.ShapeDtypeStruct((count + 128,), jnp.int32),
        name="owned",
    )(meta, labels.reshape(-1, 128))


def scaled_kernel(meta_ref, values_ref, scales_ref, scaled_ref, mine_ref):
    for h in range(2):
        at = slice(h * HALF, (h + 1) * HALF)
        values = values_ref[at, :]
        inverse = lax.rsqrt(jnp.sum(values * values, axis=1, keepdims=True) + EPS)
        scale = jnp.broadcast_to(scales_ref[2 * meta_ref[0] + h] * LOG2E, (8, HALF)).T[:, :1]
        scaled_ref[at, :] = values * (inverse * scale)
    mine_ref[...] = scaled_ref[pl.ds(pl.multiple_of(meta_ref[1] * HALF, HALF), HALF), :]


def scaled_units(meta, embeddings, scales):
    near = pl.BlockSpec(memory_space=pltpu.VMEM)
    lines, width = embeddings.shape
    return pl.pallas_call(
        scaled_kernel,
        in_specs=[pl.BlockSpec(memory_space=pltpu.SMEM), near, near],
        out_specs=[near, near],
        out_shape=[
            jax.ShapeDtypeStruct((lines, width), jnp.float32),
            jax.ShapeDtypeStruct((HALF, width), jnp.float32),
        ],
        name="scaled_units",
    )(meta, embeddings, scales)


def half_ids(meta_ref, shift, ways):
    block = lax.rem(meta_ref[0] + (ways - shift), ways)
    swap = jnp.int32(0) if shift == 0 else meta_ref[1]
    return 2 * block + swap, 2 * block + 1 - swap


def start_target(k, number, meta_ref, labels_ref, rows_ref, sources, ways, found_ref, picked_ref, sems):
    place, core, offset = meta_ref[0], meta_ref[1], meta_ref[2]
    local = labels_ref[number] - offset
    at = pl.multiple_of((local // 8) * 8, 8)
    pltpu.make_async_copy(rows_ref.at[pl.ds(at, 8), :], picked_ref.at[k], sems.at[1, k]).start()
    half = number // HALF
    shift = lax.rem(place + ways - half // 2, ways)
    swapped = jnp.where(lax.rem(half, 2) == core, 0, 1)
    for (s, w), ref in sources.items():
        here = shift == s
        if w is not None:
            here = here & (swapped == w)

        @pl.when(here)
        def _(ref=ref):
            from_row = pl.multiple_of((lax.rem(number, ref.shape[0]) // 8) * 8, 8)
            pltpu.make_async_copy(ref.at[pl.ds(from_row, 8), :], found_ref.at[k], sems.at[0, k]).start()


def stats_kernel(meta_ref, *refs, shifts, ways, first, last):
    refs = list(refs)
    take = lambda n: [refs.pop(0) for _ in range(n)]
    (labels_ref,) = take(1)
    halves = take(len(shifts) if first else 2 * len(shifts))
    if first:
        (rows_ref,) = take(1)
    else:
        high_ref, low_ref, before_ref = take(3)
    if last:
        list_ref, flat_labels_ref, flat_scales_ref, all_rows_ref = take(4)
        sources = {(0, None): refs.pop(0)}
        for s in range(1, ways):
            for w in range(2):
                sources[(s, w)] = refs.pop(0)
    (out_ref,) = take(1)
    if first:
        high_ref, low_ref = take(2)
    raw_ref, uh_ref, ul_ref, peak_ref, total_ref, local_ref, raw_sems = take(7)
    if last:
        found_ref, picked_ref, group_ref, sems = take(4)
    step = pl.program_id(0)
    offset = meta_ref[2]
    ids = [i for s in shifts for i in half_ids(meta_ref, s, ways)]

    if last:
        limit = flat_labels_ref.shape[0]

        def begin(base, here):
            def one(k, carry):
                number = list_ref[base + k]
                start_target(
                    k, number, meta_ref, flat_labels_ref, all_rows_ref, sources, ways, found_ref, picked_ref, sems
                )
                return carry

            lax.fori_loop(0, here, one, 0)

        def finish(base, here):
            def wait(k, carry):
                rows = all_rows_ref.at[pl.ds(0, 8), :]
                pltpu.make_async_copy(rows, found_ref.at[k], sems.at[0, k]).wait()
                pltpu.make_async_copy(rows, picked_ref.at[k], sems.at[1, k]).wait()
                return carry

            lax.fori_loop(0, here, wait, 0)

            def eight(g, carry):
                first_slot = g * 8
                numbers = []
                for k in range(8):
                    slot = first_slot + k
                    number = jnp.where(slot < here, list_ref[base + slot], 0)
                    local = jnp.maximum(flat_labels_ref[number] - offset, 0)
                    scaled = found_ref[slot, pl.ds(lax.rem(number, 8), 1), :]
                    group_ref[0, k : k + 1, :] = scaled / (flat_scales_ref[number] * LOG2E)
                    group_ref[1, k : k + 1, :] = picked_ref[slot, pl.ds(lax.rem(local, 8), 1), :]
                    numbers.append(number)
                units, picked = group_ref[0], group_ref[1]
                picked = picked * lax.rsqrt(jnp.sum(picked * picked, axis=1, keepdims=True) + EPS)
                cosine = jnp.sum(units * picked, axis=1, keepdims=True)
                across = units - cosine * picked
                sine = jnp.sqrt(jnp.sum(across * across, axis=1, keepdims=True))
                margin = cosine * COS_MARGIN - sine * SIN_MARGIN
                for k in range(8):
                    number = numbers[k]

                    @pl.when(first_slot + k < here)
                    def _(k=k, number=number):
                        target = flat_scales_ref[number] * margin[k : k + 1]
                        line = out_ref[number // HALF, pl.ds(1, 1), :]
                        lane = lax.broadcasted_iota(jnp.int32, line.shape, 1)
                        line = jnp.where(lane == lax.rem(number, HALF), target, line)
                        out_ref[number // HALF, pl.ds(1, 1), :] = line

                return carry

            lax.fori_loop(0, (here + 7) // 8, eight, 0)

    @pl.when(step == 0)
    def _():
        if first:
            loads = [pltpu.make_async_copy(halves[0], raw_ref, raw_sems.at[0])]
        else:
            loads = [
                pltpu.make_async_copy(ref, raw_ref.at[pl.ds(h * HALF, HALF), :], raw_sems.at[h])
                for h, ref in enumerate(halves)
            ]
        for load in loads:
            load.start()
        if last:
            begin(0, jnp.minimum(list_ref[limit], SLOTS))
        for h in range(2 * len(shifts)):
            if h < len(loads):
                loads[h].wait()
            at = slice(h * HALF, (h + 1) * HALF)
            high, low = split(raw_ref[at, :])
            uh_ref[at, :] = high
            ul_ref[at, :] = low
            local_ref[:, at] = labels_ref[ids[h]] - offset
        peak_ref[...] = jnp.full_like(peak_ref, LOWEST)
        total_ref[...] = jnp.zeros_like(total_ref)

    peak, total = peak_ref[...], total_ref[...]
    width = peak.shape[1]
    uh, ul = uh_ref[...], ul_ref[...]
    local = jnp.broadcast_to(local_ref[...] - step * TILE, (8, width))
    local = local - lax.broadcasted_iota(jnp.int32, (8, width), 0)
    for k in range(TILE // SUB):
        at = slice(k * SUB, (k + 1) * SUB)
        if first:
            rows = rows_ref[at, :]
            rows = rows * lax.rsqrt(jnp.sum(rows * rows, axis=1, keepdims=True) + EPS)
            high, low = split(rows)
            high_ref[at, :] = high
            low_ref[at, :] = low
        else:
            high, low = high_ref[at, :], low_ref[at, :]
        logits = product(high, uh) + product(low, uh) + product(high, ul)
        parts = [
            jnp.where(local == k * SUB + 8 * g, LOWEST, logits[8 * g : 8 * g + 8]) for g in range(SUB // 8)
        ]
        tops = list(parts)
        while len(tops) > 1:
            tops = [jnp.maximum(a, b) for a, b in zip(tops[::2], tops[1::2])]
        above = jnp.maximum(peak, tops[0])
        sums = [jnp.exp2(part - above) for part in parts]
        while len(sums) > 1:
            sums = [a + b for a, b in zip(sums[::2], sums[1::2])]
        total = total * jnp.exp2(peak - above) + sums[0]
        peak = above
    peak_ref[...] = peak
    total_ref[...] = total

    @pl.when(step == pl.num_programs(0) - 1)
    def _():
        top = jnp.max(peak, axis=0, keepdims=True)
        full = jnp.sum(total * jnp.exp2(peak - top), axis=0, keepdims=True)
        level = top + jnp.log2(full)
        if first:
            out_ref[...] = jnp.zeros_like(out_ref)
        else:
            out_ref[...] = before_ref[...]
        for h, i in enumerate(ids):
            out_ref[i, pl.ds(0, 1), :] = level[:, h * HALF : (h + 1) * HALF]
        if last:
            found = list_ref[limit]
            finish(0, jnp.minimum(found, SLOTS))

            def batch(b, carry):
                here = jnp.minimum(found - b * SLOTS, SLOTS)
                begin(b * SLOTS, here)
                finish(b * SLOTS, here)
                return carry

            lax.fori_loop(1, (found + SLOTS - 1) // SLOTS, batch, 0)


def stats(meta, labels, shifts, halves, rows, ways, before=None, extra=None):
    first, last = before is None, extra is not None
    rows_here, width = rows[0].shape
    blocks = labels.shape[0]
    lines = 2 * HALF * len(shifts)
    whole = lambda *shape: pl.BlockSpec(shape, lambda t, meta: (0,) * len(shape))
    far = pl.BlockSpec(memory_space=pl.ANY)
    scalars = pl.BlockSpec(memory_space=pltpu.SMEM)
    tiles = pl.BlockSpec((TILE, width), lambda t, meta: (t, 0))
    in_specs = [whole(blocks, 1, HALF)] + [far] * len(halves) + [tiles] * len(rows)
    args = [labels, *halves, *rows]
    out_specs = [whole(blocks, 2, HALF)]
    out_shape = [jax.ShapeDtypeStruct((blocks, 2, HALF), jnp.float32)]
    scratch = [
        pltpu.VMEM((lines, width), jnp.float32),
        pltpu.VMEM((lines, width), jnp.bfloat16),
        pltpu.VMEM((lines, width), jnp.bfloat16),
        pltpu.VMEM((8, lines), jnp.float32),
        pltpu.VMEM((8, lines), jnp.float32),
        pltpu.VMEM((1, lines), jnp.int32),
        pltpu.SemaphoreType.DMA((2 * len(shifts),)),
    ]
    if first:
        out_specs += [tiles, tiles]
        out_shape += [jax.ShapeDtypeStruct((rows_here, width), jnp.bfloat16)] * 2
    else:
        in_specs.append(whole(blocks, 2, HALF))
        args.append(before)
    if last:
        in_specs += [scalars] * 3 + [far] * (len(extra) - 3)
        args += extra
        scratch += [
            pltpu.VMEM((SLOTS, 8, width), jnp.float32),
            pltpu.VMEM((SLOTS, 8, width), jnp.float32),
            pltpu.VMEM((2, 8, width), jnp.float32),
            pltpu.SemaphoreType.DMA((2, SLOTS)),
        ]
    return pl.pallas_call(
        functools.partial(stats_kernel, shifts=shifts, ways=ways, first=first, last=last),
        grid_spec=pltpu.PrefetchScalarGridSpec(
            num_scalar_prefetch=1,
            grid=(rows_here // TILE,),
            in_specs=in_specs,
            out_specs=out_specs,
            scratch_shapes=scratch,
        ),
        out_shape=out_shape,
        compiler_params=pltpu.CompilerParams(dimension_semantics=("arbitrary",)),
    )(meta, *args)


def body(embeddings, classifier, labels, row_scale):
    rows_here = classifier.shape[0]
    count = labels.shape[0]
    ways = lax.axis_size("dp")
    core = lax.axis_index("cls_2")
    meta = jnp.stack([lax.axis_index("dp"), core, lax.axis_index(DP_CLS) * rows_here]).astype(jnp.int32)
    swap = lambda part: lax.ppermute(part, "cls_2", [(0, 1), (1, 0)])
    shift = lambda part, k: lax.ppermute(part, "dp", [(i, (i + k) % ways) for i in range(ways)])

    label_blocks = labels.reshape(-1, 1, HALF)
    scale_blocks = row_scale.reshape(-1, 1, HALF)
    scaled, mine = scaled_units(meta, embeddings, scale_blocks)
    left = shift(mine, 1)
    right = shift(mine, 3)
    across = shift(mine, 2)
    numbers = owned(meta, labels, rows_here)
    held, high, low = stats(meta, label_blocks, (0,), (scaled,), (classifier,), ways)
    left_other = swap(left)
    near = (left, left_other, right, swap(right))
    (held,) = stats(meta, label_blocks, (1, 3), near, (high, low), ways, held)
    across_other = swap(across)
    far = (across, across_other)
    extra = [numbers, labels, row_scale, classifier, scaled, near[0], near[1], *far, near[2], near[3]]
    (held,) = stats(meta, label_blocks, (2,), far, (high, low), ways, held, extra)

    devices = lax.axis_size(DP_CLS)
    share = count // devices
    send = held.reshape(-1, 2, HALF // share, share).transpose(0, 2, 1, 3).reshape(devices, 2 * share)
    got = lax.all_to_all(send, DP_CLS, 0, 0, tiled=True)
    level, target = got[:, :share], jnp.sum(got[:, share:], axis=0)
    top = jnp.max(level, axis=0)
    peak = jnp.maximum(top * LN2, target)
    total = jnp.sum(jnp.exp2(level - top), axis=0) * jnp.exp(top * LN2 - peak) + jnp.exp(target - peak)
    return peak + jnp.log(total) - target


def solution(mesh):
    torus = Mesh(mesh.devices.reshape(mesh.shape["dp"], 8, 4, 2), ("dp", "cls_0", "cls_1", "cls_2"))
    return jax.shard_map(
        body,
        mesh=torus,
        in_specs=(P("dp", None), P(DP_CLS, None), P(), P()),
        out_specs=P(DP_CLS),
        check_vma=False,
    )
```
